32 devices in a mesh: grp: 8 (over z, core), reg: 4 (over y, x).
Axes of the slice: x: 2, y: 2, z: 4, core: 2. Of those that a mesh axis runs over, the one named last changes fastest.
Arguments:
- queries: bfloat16 [4096, 1536], P(('grp', 'reg')), parts along dimension 0, may hold values from -9 to 9
- keys_now: bfloat16 [4096, 1536], P(('grp', 'reg')), parts along dimension 0, may hold values from -9 to 9
- values_now: bfloat16 [4096, 1536], P(('grp', 'reg')), parts along dimension 0, may hold values from -6 to 6
- keys_stale: bfloat16 [4096, 1536], P(('grp', 'reg')), parts along dimension 0, may hold values from -9 to 9
- values_stale: bfloat16 [4096, 1536], P(('grp', 'reg')), parts along dimension 0, may hold values from -6 to 6
- neighbours: int32 [32, 2], P('grp'), parts along dimension 0, may hold values from -1 to 3, as said below
Outputs:
- attended: bfloat16 [4096, 1536], P(('grp', 'reg')), parts along dimension 0
The draws below stay inside these ranges and needn't reach their ends.
There are 8 independent parts, one for each index of `grp`. The reference program is written for one: setup_inputs(seed, part) draws one part's arguments, and reference() takes and returns one part's arrays. A program takes and returns all parts, laid end to end along the dimension named above; each array names one. Nothing has to cross between parts.
Inputs may be any that keep to these rules, and one draw needn't show every extreme that they name: `neighbours`: row r holds first between 1 and 2 distinct region numbers other than r, then -1 in its remaining slots; some row holds 2 numbers.
All inputs are finite; a program needn't handle non-finite values.
Results may differ from the reference program's by a relative error of at most 0.0085.
Values may be sent and summed in bfloat16 or wider, within the bound.
No kernel may reach another device: no remote copies, remote signals or barrier semaphores. Data moves between devices by JAX's collectives and lax.ppermute only.
A program may use at most 128 MiB of HBM per device.

```python
import jax
import jax.numpy as jnp
from jax import lax

HEADS = 12
HD = 128
TOK_DEV = 128
HALO = 128
TOKENS = 512
F = 1536
N_REG = 4


def neighbour_table(key):
    base = jax.random.fold_in(key, 777)
    key_perm, key_long, key_base = jax.random.split(base, 3)
    slot_count = N_REG // 2

    def one_row(region):
        shuffled = jax.random.permutation(jax.random.fold_in(key_perm, region), N_REG)
        order = jnp.argsort((shuffled == region).astype(jnp.int32), stable=True)
        return shuffled[order][:slot_count]
    lists = jax.vmap(one_row)(jnp.arange(N_REG, dtype=jnp.int32))
    longest = jax.random.randint(key_long, (2,), 0, N_REG)
    counts = 1 + jax.random.randint(key_base, (N_REG,), 0, 2)
    counts = jnp.minimum(counts, slot_count).at[longest].set(slot_count)
    columns = jnp.arange(slot_count, dtype=jnp.int32)
    return jnp.where(columns[None, :] < counts[:, None], lists, -1).astype(jnp.int32)


def joint_draw(key):
    base = jax.random.fold_in(key, 4242)
    key_query = jax.random.fold_in(base, 0)
    key_keys = jax.random.fold_in(base, 1)
    key_stale = jax.random.fold_in(base, 5)
    width = HEADS * HD
    total_rows = TOK_DEV * N_REG
    query_vals = 1.5 * jnp.clip(jax.random.normal(key_query, (total_rows, width), jnp.float32), -6.0, 6.0)
    key_vals = jnp.clip(jax.random.normal(key_keys, (total_rows, width), jnp.float32), -6.0, 6.0)
    stale_vals = jnp.clip(jax.random.normal(key_stale, (total_rows, width), jnp.float32), -6.0, 6.0)
    return (query_vals, key_vals, stale_vals)


def draw_queries(key, part):
    return joint_draw(key)[0].astype(jnp.bfloat16)


def draw_keys_now(key, part):
    return joint_draw(key)[1].astype(jnp.bfloat16)


def draw_keys_stale(key, part):
    return joint_draw(key)[2].astype(jnp.bfloat16)


def draw_neighbours(key, part):
    return neighbour_table(key)


def block_levels(stream_key, shape, cuts, low, top_value):
    gain = 1.0
    for axis_at, blocks in cuts:
        steps = jax.random.uniform(jax.random.fold_in(jax.random.fold_in(stream_key, 6), axis_at), (blocks,), jnp.float32, low / len(cuts), top_value / len(cuts))
        gain = gain * jnp.repeat(jnp.exp(steps), shape[axis_at] // blocks).reshape((-1,) + (1,) * (len(shape) - 1 - axis_at))
    return gain


def centred(rng, shape, spread, limit, cuts=(), kind=jnp.bfloat16):
    level = block_levels(rng, shape, cuts, -0.22, 0.18) if cuts else 1.0
    drawn = jax.random.normal(rng, shape, jnp.float32) * spread * level
    return jnp.minimum(jnp.maximum(drawn, -limit), limit).astype(kind)


def setup_inputs(seed: int = 0, part: int = 0) -> dict:
    key_of = jax.random.split(jax.random.key(seed), 7)
    part_keys = jax.random.split(jax.random.fold_in(key_of[6], part), 7)
    return {
        "queries": draw_queries(jax.random.fold_in(jax.random.fold_in(key_of[6], part), 71), part),
        "keys_now": draw_keys_now(jax.random.fold_in(jax.random.fold_in(key_of[6], part), 71), part),
        "values_now": centred(part_keys[2], (TOKENS, F), 1.0, 6.0, ((0, 4),)),
        "keys_stale": draw_keys_stale(jax.random.fold_in(jax.random.fold_in(key_of[6], part), 71), part),
        "values_stale": centred(part_keys[4], (TOKENS, F), 1.0, 6.0, ((0, 4),)),
        "neighbours": draw_neighbours(jax.random.fold_in(jax.random.fold_in(key_of[6], part), 71), part),
    }


def block_partial(query_rows, key_rows, value_rows, key_valid):
    rows = query_rows.shape[0]
    count = key_rows.shape[0]
    query3 = query_rows.reshape(rows, HEADS, HD).astype(jnp.float32)
    key3 = key_rows.reshape(count, HEADS, HD).astype(jnp.float32)
    value3 = value_rows.reshape(count, HEADS, HD).astype(jnp.float32)
    scores = jnp.einsum('thd,shd->ths', query3, key3) * (HD ** -0.5)
    scores = jnp.where(key_valid[None, None, :], scores, -jnp.inf)
    peak = jnp.max(scores, axis=-1)
    weights = jnp.exp(scores - peak[..., None])
    total = jnp.sum(weights, axis=-1)
    rounded = weights.astype(jnp.bfloat16).astype(jnp.float32)
    numer = jnp.einsum('ths,shd->thd', rounded, value3)
    partial_out = (numer / total[..., None]).reshape(rows, HEADS * HD).astype(jnp.bfloat16)
    return peak, total, partial_out


def reference(queries, keys_now, values_now, keys_stale, values_stale, neighbours):
    total_rows = TOK_DEV * N_REG
    span = TOK_DEV + 2 * HALO
    keys_pad = jnp.pad(keys_now, ((HALO, HALO), (0, 0)))
    values_pad = jnp.pad(values_now, ((HALO, HALO), (0, 0)))
    owners = jnp.arange(N_REG, dtype=jnp.int32)

    def one_region(region):
        start = (region * TOK_DEV).astype(jnp.int32)
        query_rows = lax.dynamic_slice_in_dim(queries, start, TOK_DEV, 0)
        local_keys = lax.dynamic_slice_in_dim(keys_pad, start, span, 0)
        local_values = lax.dynamic_slice_in_dim(values_pad, start, span, 0)
        position = start - HALO + jnp.arange(span, dtype=jnp.int32)
        valid = (position >= 0) & (position < total_rows)
        peak_local, total_local, out_local = block_partial(query_rows, local_keys, local_values, valid)
        own_list = neighbours[region]
        member = jnp.any(own_list[:, None] == owners[None, :], axis=0)

        def one_owner(owner):
            begin = (owner * TOK_DEV).astype(jnp.int32)
            key_rows = lax.dynamic_slice_in_dim(keys_stale, begin, TOK_DEV, 0)
            value_rows = lax.dynamic_slice_in_dim(values_stale, begin, TOK_DEV, 0)
            return block_partial(query_rows, key_rows, value_rows, jnp.ones((TOK_DEV,), bool))

        peaks, totals, outs = lax.map(one_owner, owners)
        masked_peaks = jnp.where(member[:, None, None], peaks, -jnp.inf)
        top = jnp.maximum(peak_local, jnp.max(masked_peaks, axis=0))
        weight_local = jnp.exp(peak_local - top) * total_local
        weights = jnp.where(member[:, None, None], jnp.exp(masked_peaks - top) * totals, 0.0)
        denom = weight_local + jnp.sum(weights, axis=0)
        numer = weight_local[..., None] * out_local.astype(jnp.float32).reshape(TOK_DEV, HEADS, HD)
        numer = numer + jnp.einsum('nth,nthd->thd', weights, outs.astype(jnp.float32).reshape(N_REG, TOK_DEV, HEADS, HD))
        return (numer / denom[..., None]).reshape(TOK_DEV, HEADS * HD).astype(jnp.bfloat16)

    result = lax.map(one_region, owners)
    return result.reshape(total_rows, HEADS * HD)
```

```python
import functools
import math

import jax
import jax.numpy as jnp
from jax import lax
from jax.experimental import pallas as pl
from jax.experimental.pallas import tpu as pltpu
from jax.sharding import PartitionSpec as P

HD = 128
LANES = 128
PIECE_ROWS = 16
NEVER = -1e30
SCALE2 = HD**-0.5 * math.log2(math.e)


def grid_shape(count):
    rows = max(d for d in range(1, math.isqrt(count) + 1) if count % d == 0)
    return rows, count // rows


def groups_of(count, by_row):
    rows, cols = grid_shape(count)
    across, down = [], []
    for r in range(count):
        y, x = divmod(r, cols)
        across.append([y * cols + (x + s) % cols for s in range(cols)])
        down.append([((y + s) % rows) * cols + x for s in range(rows)])
    return (across, down) if by_row else (down, across)


def near(a, b):
    return abs(a - b) <= 1


def attend_kernel(n_visit, n_share, heads, rows, *refs):
    valid = refs[0]
    refs = refs[1:]
    queries, refs = refs[:n_visit], refs[n_visit:]
    own, refs = refs[:4], refs[4:]
    shared, refs = refs[: 2 * (n_share - 1)], refs[2 * (n_share - 1) :]
    out_own, lse_own = refs[:2]
    messages = refs[2:]
    total_rows = n_visit * rows
    row = lax.broadcasted_iota(jnp.int32, (total_rows, 1), 0)

    def bias_of(block):
        column = jnp.full((total_rows, 1), NEVER, jnp.float32)
        for v in range(n_visit):
            value = jnp.where(valid[v * 2 * n_share + block] != 0, 0.0, NEVER).astype(jnp.float32)
            column = jnp.where((row >= v * rows) & (row < (v + 1) * rows), value, column)
        return column

    biases = [bias_of(b) for b in range(2 * n_share)]
    lane = lax.broadcasted_iota(jnp.int32, (rows, LANES), 1)
    lse_all = [jnp.zeros((rows, LANES), jnp.float32) for _ in range(n_visit)]
    for h in range(heads):
        cols = slice(h * HD, (h + 1) * HD)
        q = jnp.concatenate([ref[:, cols] for ref in queries], axis=0)
        keys = [own[0][:, cols], own[2][:, cols]]
        values = [own[1][:, cols], own[3][:, cols]]
        for s in range(n_share - 1):
            keys += [shared[2 * s][0, :, cols], shared[2 * s + 1][0, :, cols]]
            values += [shared[2 * s][1, :, cols], shared[2 * s + 1][1, :, cols]]
        scores = [
            lax.dot_general(q, k, (((1,), (1,)), ((), ())), preferred_element_type=jnp.float32) + b
            for k, b in zip(keys, biases)
        ]
        peak = functools.reduce(jnp.maximum, scores).max(axis=1, keepdims=True)
        weights = [jnp.exp2((s - peak) * SCALE2) for s in scores]
        total = functools.reduce(jnp.add, weights).sum(axis=1, keepdims=True)
        numer = functools.reduce(
            jnp.add,
            [
                jnp.dot(w.astype(jnp.bfloat16), v, preferred_element_type=jnp.float32)
                for w, v in zip(weights, values)
            ],
        )
        out = (numer / total).astype(jnp.bfloat16)
        lse = peak * SCALE2 + jnp.log2(total)
        out_own[:, cols] = out[:rows]
        for v in range(n_visit):
            lse_all[v] = jnp.where(lane == h, lse[v * rows : (v + 1) * rows], lse_all[v])
            if v:
                messages[v - 1][:rows, cols] = out[v * rows : (v + 1) * rows]
    lse_own[...] = lse_all[0]
    piece = lax.broadcasted_iota(jnp.int32, (PIECE_ROWS, rows), 0)
    for v in range(1, n_visit):
        flat = lse_all[v].T
        for h in range(heads):
            line = flat[h : h + 1, :]
            high = line.astype(jnp.bfloat16)
            rest = line - high.astype(jnp.float32)
            middle = rest.astype(jnp.bfloat16)
            low = (rest - middle.astype(jnp.float32)).astype(jnp.bfloat16)
            tile = jnp.where(
                piece == 0,
                high.astype(jnp.float32),
                jnp.where(piece == 1, middle.astype(jnp.float32), low.astype(jnp.float32)),
            )
            messages[v - 1][rows:, h * HD : (h + 1) * HD] = tile.astype(jnp.bfloat16)


def merge_kernel(n_visit, chunks, rows, *refs):
    out = refs[-1]
    at = 0
    for first, heads in chunks:
        part, lse_own = refs[at], refs[at + 1]
        messages = refs[at + 2 : at + 1 + n_visit]
        at += 1 + n_visit
        columns = []
        for message in messages:
            lines = []
            for h in range(heads):
                tile = message[rows:, h * HD : (h + 1) * HD].astype(jnp.float32)
                lines.append(tile[0:1] + tile[1:2] + tile[2:3])
            flat = jnp.concatenate(lines + [jnp.zeros((LANES - heads, rows), jnp.float32)], axis=0)
            columns.append(flat.T)
        for h in range(heads):
            cols = slice(h * HD, (h + 1) * HD)
            lses = [lse_own[:, h : h + 1]] + [c[:, h : h + 1] for c in columns]
            parts = [part[:, cols]] + [m[:rows, cols] for m in messages]
            top = functools.reduce(jnp.maximum, lses)
            weights = [jnp.exp2(l - top) for l in lses]
            denom = functools.reduce(jnp.add, weights)
            numer = functools.reduce(
                jnp.add, [w * p.astype(jnp.float32) for w, p in zip(weights, parts)]
            )
            out[:, (first + h) * HD : (first + h + 1) * HD] = (numer / denom).astype(jnp.bfloat16)


def plan_of(heads):
    half = heads // 2
    step = max(1, half // 2)
    plan = []
    for at in range(0, half, step):
        plan.append((at, min(step, half - at), True))
        plan.append((half + at, min(step, heads - half - at), False))
    return plan


def on_device(count, queries, keys_now, values_now, keys_stale, values_stale, neighbours):
    region = lax.axis_index("reg")
    rows, width = queries.shape
    plan = plan_of(width // HD)
    owners = jnp.arange(count, dtype=jnp.int32)
    member = jnp.any(neighbours[:, :, None] == owners[None, None, :], axis=1)
    beside = jnp.abs(owners[:, None] - owners[None, :]) <= 1

    def cut(x, first, heads):
        return lax.slice_in_dim(x, first * HD, (first + heads) * HD, axis=1)

    travelled = []
    for first, heads, by_row in plan:
        share, visit = groups_of(count, by_row)
        q = cut(queries, first, heads)
        stale = jnp.stack([cut(keys_stale, first, heads), cut(values_stale, first, heads)])
        now = jnp.stack([cut(keys_now, first, heads), cut(values_now, first, heads)])
        visiting = [q]
        for s in range(1, len(visit[0])):
            visiting.append(lax.ppermute(q, "reg", [(visit[d][s], d) for d in range(count)]))
        shared = []
        for s in range(1, len(share[0])):
            pairs = [(share[d][s], d) for d in range(count)]
            needed = [(m, d) for m, d in pairs if any(near(q_of, m) for q_of in visit[d])]
            shared.append(lax.ppermute(now, "reg", needed))
            shared.append(lax.ppermute(stale, "reg", pairs))
        travelled.append((visiting, shared))

    results = []
    for (first, heads, by_row), (visiting, shared) in zip(plan, travelled):
        share, visit = groups_of(count, by_row)
        n_visit, n_share = len(visit[0]), len(share[0])
        share_here = jnp.asarray(share, jnp.int32)[region]
        visit_here = jnp.asarray(visit, jnp.int32)[region]
        table = jnp.stack([beside, member], axis=-1)
        valid = table[visit_here][:, share_here].astype(jnp.int32).reshape(-1)
        chunk = heads * HD
        block = first // heads
        assert first % heads == 0
        whole = lambda x: pl.BlockSpec(x.shape, lambda _, n=x.ndim: (0,) * n)
        column = pl.BlockSpec((rows, chunk), lambda _, block=block: (0, block))
        operands = visiting[1:]
        outs = pl.pallas_call(
            functools.partial(attend_kernel, n_visit, n_share, heads, rows),
            grid=(1,),
            in_specs=[pl.BlockSpec(memory_space=pltpu.SMEM), column]
            + [whole(x) for x in operands]
            + [column] * 4
            + [whole(x) for x in shared],
            out_specs=[
                pl.BlockSpec((rows, chunk), lambda _: (0, 0)),
                pl.BlockSpec((rows, LANES), lambda _: (0, 0)),
            ]
            + [pl.BlockSpec((rows + PIECE_ROWS, chunk), lambda _: (0, 0))] * (n_visit - 1),
            out_shape=[
                jax.ShapeDtypeStruct((rows, chunk), jnp.bfloat16),
                jax.ShapeDtypeStruct((rows, LANES), jnp.float32),
            ]
            + [jax.ShapeDtypeStruct((rows + PIECE_ROWS, chunk), jnp.bfloat16)] * (n_visit - 1),
            name="attend",
        )(valid, queries, *operands, keys_now, values_now, keys_stale, values_stale, *shared)
        own, messages = outs[:2], outs[2:]
        back = [
            lax.ppermute(m, "reg", [(d, visit[d][s + 1]) for d in range(count)])
            for s, m in enumerate(messages)
        ]
        results.append((own, back))

    flat = []
    for own, back in results:
        flat += [*own, *back]
    n_visit = 1 + len(results[0][1])
    return pl.pallas_call(
        functools.partial(merge_kernel, n_visit, [(f, h) for f, h, _ in plan], rows),
        out_shape=jax.ShapeDtypeStruct((rows, width), jnp.bfloat16),
        name="merge",
    )(*flat)


def solution(mesh):
    in_specs = (
        P(("grp", "reg"), None),
        P(("grp", "reg"), None),
        P(("grp", "reg"), None),
        P(("grp", "reg"), None),
        P(("grp", "reg"), None),
        P("grp", None),
    )
    out_specs = P(("grp", "reg"), None)
    return jax.shard_map(
        functools.partial(on_device, mesh.shape["reg"]),
        mesh=mesh,
        in_specs=in_specs,
        out_specs=out_specs,
        check_vma=False,
    )
```

```python
import functools
import math

import jax
import jax.numpy as jnp
from jax import lax
from jax.experimental import pallas as pl
from jax.experimental.pallas import tpu as pltpu
from jax.sharding import PartitionSpec as P

HD = 128
LANES = 128
TILE_ROWS = 16
NEVER = -1e30
VMEM_BUDGET = 2 << 20
SCALE2 = HD**-0.5 * math.log2(math.e)


def grid_shape(count):
    rows = max(d for d in range(1, math.isqrt(count) + 1) if count % d == 0)
    return rows, count // rows


def neighbour_of(region, shift, across, shape):
    rows, cols = shape
    y, x = region // cols, region % cols
    if across:
        return y * cols + (x + shift) % cols
    return ((y + shift) % rows) * cols + x


def pairs_of(count, shift, across, shape):
    return [(neighbour_of(d, shift, across, shape), d) for d in range(count)]


def reversed_pairs(pairs):
    return [(d, s) for s, d in pairs]


def padded(n):
    return -(-n // TILE_ROWS) * TILE_ROWS


class Chunk:
    def __init__(self, first, heads, across, visit_at):
        self.first, self.heads, self.across, self.visit_at = first, heads, across, visit_at

    def sizes(self, shape):
        rows, cols = shape
        return (rows, cols) if self.across else (cols, rows)

    def message_rows(self, rows):
        return self.heads * rows + padded(3 * self.heads)


def attend_kernel(chunk, count, shape, n_visit, n_share, rows, *refs):
    listed = refs[0]
    queries = refs[1 : 1 + n_visit]
    own = refs[1 + n_visit : 5 + n_visit]
    shared = refs[5 + n_visit : 4 + n_visit + n_share]
    out_own, lse_own = refs[4 + n_visit + n_share : 6 + n_visit + n_share]
    messages = refs[6 + n_visit + n_share :]
    heads = chunk.heads
    region = lax.axis_index("reg")
    slots = listed.shape[1]

    def block_bias(v, s, stale):
        ids = [
            (neighbour_of(d, v, not chunk.across, shape), neighbour_of(d, s, chunk.across, shape))
            for d in range(count)
        ]
        if stale:
            if all(q == m for q, m in ids):
                return False
            query_region = neighbour_of(region, v, not chunk.across, shape)
            key_region = neighbour_of(region, s, chunk.across, shape)
            hit = listed[query_region, 0] == key_region
            for j in range(1, slots):
                hit = hit | (listed[query_region, j] == key_region)
        else:
            close = [abs(q - m) <= 1 for q, m in ids]
            if all(close):
                return None
            if not any(close):
                return False
            hit = functools.reduce(
                jnp.logical_or, [region == d for d in range(count) if close[d]]
            )
        return jnp.where(hit, 0.0, NEVER).astype(jnp.float32)

    blocks = [
        [
            (s, stale, bias)
            for s in range(n_share)
            for stale in (0, 1)
            for bias in [block_bias(v, s, stale)]
            if bias is not False
        ]
        for v in range(n_visit)
    ]
    lane = lax.broadcasted_iota(jnp.int32, (rows, LANES), 1)
    lse_all = [jnp.zeros((rows, LANES), jnp.float32) for _ in range(n_visit)]
    for h in range(heads):
        here = slice((chunk.first + h) * HD, (chunk.first + h + 1) * HD)
        there = slice(h * HD, (h + 1) * HD)
        visiting = slice((chunk.visit_at + h) * HD, (chunk.visit_at + h + 1) * HD)

        def load(s, stale, value):
            if s == 0:
                return own[2 * stale + value][:, here]
            return shared[s - 1][2 * stale + value, :, there]

        for v in range(n_visit):
            q = queries[v][:, visiting] if v else queries[0][:, here]
            keys = jnp.concatenate([load(s, t, 0) for s, t, _ in blocks[v]], axis=0)
            values = jnp.concatenate([load(s, t, 1) for s, t, _ in blocks[v]], axis=0)
            values = jnp.concatenate(
                [values, jnp.ones((values.shape[0], LANES), jnp.bfloat16)], axis=1
            )
            scores = lax.dot_general(
                q, keys, (((1,), (1,)), ((), ())), preferred_element_type=jnp.float32
            )
            pieces = []
            for i, (_, _, bias) in enumerate(blocks[v]):
                piece = scores[:, i * rows : (i + 1) * rows]
                pieces.append(piece if bias is None else piece + bias)
            peak = functools.reduce(jnp.maximum, pieces).max(axis=1, keepdims=True) * SCALE2
            weights = [jnp.exp2(p * SCALE2 - peak).astype(jnp.bfloat16) for p in pieces]
            both = jnp.dot(
                jnp.concatenate(weights, axis=1), values, preferred_element_type=jnp.float32
            )
            total = both[:, HD:]
            out = (both[:, :HD] / total).astype(jnp.bfloat16)
            lse_all[v] = jnp.where(lane == h, peak + jnp.log2(total), lse_all[v])
            if v == 0:
                out_own[:, there] = out
            else:
                messages[v - 1][h * rows : (h + 1) * rows, :] = out
    lse_own[...] = lse_all[0].T[: padded(heads)]
    for v in range(1, n_visit):
        flat = lse_all[v].T[: padded(heads)]
        high = flat.astype(jnp.bfloat16).astype(jnp.float32)
        middle = (flat - high).astype(jnp.bfloat16).astype(jnp.float32)
        low = flat - high - middle
        lines = [x[:heads] for x in (high, middle, low)]
        spare = padded(3 * heads) - 3 * heads
        if spare:
            lines.append(jnp.zeros((spare, rows), jnp.float32))
        messages[v - 1][heads * rows :, :] = jnp.concatenate(lines, axis=0).astype(jnp.bfloat16)


def merge_kernel(chunks, n_visits, rows, *refs):
    first = min(c.first for c in chunks)
    buffer, sem = refs[-2:]
    out = refs[-3]
    at = 0
    for chunk, n_visit in zip(chunks, n_visits):
        heads = chunk.heads
        part, lse_own = refs[at], refs[at + 1]
        messages = refs[at + 2 : at + 1 + n_visit]
        at += 1 + n_visit
        flats = [lse_own[:heads]]
        for message in messages:
            lines = message[heads * rows :, :].astype(jnp.float32)
            flats.append(
                lines[:heads] + lines[heads : 2 * heads] + lines[2 * heads : 3 * heads]
            )
        top = functools.reduce(jnp.maximum, flats)
        weights = [jnp.exp2(f - top) for f in flats]
        denom = functools.reduce(jnp.add, weights)
        blank = jnp.zeros((LANES - heads, rows), jnp.float32)
        columns = [jnp.concatenate([w / denom, blank], axis=0).T for w in weights]
        for h in range(heads):
            cols = slice(h * HD, (h + 1) * HD)
            parts = [part[:, cols]] + [m[h * rows : (h + 1) * rows, :] for m in messages]
            value = functools.reduce(
                jnp.add,
                [c[:, h : h + 1] * p.astype(jnp.float32) for c, p in zip(columns, parts)],
            )
            to = chunk.first - first + h
            buffer[:, to * HD : (to + 1) * HD] = value.astype(jnp.bfloat16)
    width = sum(c.heads for c in chunks) * HD
    copy = pltpu.make_async_copy(buffer, out.at[:, first * HD : first * HD + width], sem)
    copy.start()
    copy.wait()


def plan_of(heads):
    half = heads // 2
    later = max(1, half // 3)
    early = half - later
    stages = []
    at = 0
    for n, visit_at in ((early, 0), (later, early)):
        if n:
            stages.append([Chunk(at, n, True, visit_at), Chunk(at + n, n, False, visit_at)])
            at += 2 * n
    return stages


def placement(resident):
    if resident:
        return (
            lambda x: pltpu.with_memory_space_constraint(x, pltpu.VMEM),
            lambda shape, dtype: pltpu.VMEM(shape, dtype),
        )
    return lambda x: x, jax.ShapeDtypeStruct


def on_device(count, queries, keys_now, values_now, keys_stale, values_stale, neighbours):
    rows, width = queries.shape
    shape = grid_shape(count)
    stages = plan_of(width // HD)
    chunks = [c for stage in stages for c in stage]
    assert sum(c.heads for c in chunks) * HD == width

    def cut(x, chunk):
        return lax.slice_in_dim(x, chunk.first * HD, (chunk.first + chunk.heads) * HD, axis=1)

    arriving = sum((c.sizes(shape)[1] - 1) * 4 * rows * c.heads * HD * 2 for c in chunks)
    in_vmem, result = placement(arriving <= VMEM_BUDGET)

    visiting = {}
    for across in (True, False):
        q = jnp.concatenate([cut(queries, c) for c in chunks if c.across == across], axis=1)
        n_visit = chunks[0].sizes(shape)[0] if across else chunks[1].sizes(shape)[0]
        visiting[across] = [
            lax.ppermute(q, "reg", pairs_of(count, v, not across, shape))
            for v in range(1, n_visit)
        ]
    shared = []
    for chunk in chunks:
        mine = jnp.stack(
            [cut(x, chunk) for x in (keys_now, values_now, keys_stale, values_stale)]
        )
        shared.append(
            [
                lax.ppermute(mine, "reg", pairs_of(count, s, chunk.across, shape))
                for s in range(1, chunk.sizes(shape)[1])
            ]
        )

    local = [in_vmem(x) for x in (keys_now, values_now, keys_stale, values_stale)]
    vmem = pl.BlockSpec(memory_space=pltpu.VMEM)
    results = []
    for chunk, keys in zip(chunks, shared):
        n_visit, n_share = chunk.sizes(shape)
        outs = pl.pallas_call(
            functools.partial(attend_kernel, chunk, count, shape, n_visit, n_share, rows),
            in_specs=[pl.BlockSpec(memory_space=pltpu.SMEM)] + [vmem] * (4 + n_visit + n_share - 1),
            out_specs=[vmem] * (1 + n_visit),
            out_shape=[
                result((rows, chunk.heads * HD), jnp.bfloat16),
                result((padded(chunk.heads), rows), jnp.float32),
            ]
            + [result((chunk.message_rows(rows), HD), jnp.bfloat16)] * (n_visit - 1),
            name="attend",
        )(
            neighbours,
            in_vmem(queries),
            *[in_vmem(q) for q in visiting[chunk.across]],
            *local,
            *[in_vmem(k) for k in keys],
        )
        back = [
            lax.ppermute(
                message, "reg", reversed_pairs(pairs_of(count, v + 1, not chunk.across, shape))
            )
            for v, message in enumerate(outs[2:])
        ]
        results.append([outs[0], outs[1], *back])

    out = None
    at = 0
    for stage in stages:
        operands = []
        for chunk in stage:
            operands += [in_vmem(x) for x in results[at]]
            at += 1
        stage_width = sum(c.heads for c in stage) * HD
        n_visits = [c.sizes(shape)[0] for c in stage]
        anywhere = pl.BlockSpec(memory_space=pl.ANY)
        kernel = functools.partial(merge_kernel, stage, n_visits, rows)
        if out is not None:
            body = kernel
            kernel = lambda old, *refs, body=body: body(*refs)
        out = pl.pallas_call(
            kernel,
            in_specs=([anywhere] if out is not None else []) + [vmem] * len(operands),
            out_specs=anywhere,
            out_shape=jax.ShapeDtypeStruct((rows, width), jnp.bfloat16),
            scratch_shapes=[
                pltpu.VMEM((rows, stage_width), jnp.bfloat16),
                pltpu.SemaphoreType.DMA,
            ],
            input_output_aliases={0: 0} if out is not None else {},
            name="merge",
        )(*([out] if out is not None else []), *operands)
    return out


def solution(mesh):
    in_specs = (
        P(("grp", "reg"), None),
        P(("grp", "reg"), None),
        P(("grp", "reg"), None),
        P(("grp", "reg"), None),
        P(("grp", "reg"), None),
        P("grp", None),
    )
    out_specs = P(("grp", "reg"), None)
    return jax.shard_map(
        functools.partial(on_device, mesh.shape["reg"]),
        mesh=mesh,
        in_specs=in_specs,
        out_specs=out_specs,
        check_vma=False,
    )
```

```python
import functools
import math

import jax
import jax.numpy as jnp
from jax import lax
from jax.experimental import pallas as pl
from jax.experimental.pallas import tpu as pltpu
from jax.sharding import PartitionSpec as P

HD = 128
LANES = 128
TILE_ROWS = 16
NEVER = -1e30
VMEM_BUDGET = 2 << 20
KERNEL_VMEM = 2 << 20
SCALE2 = HD**-0.5 * math.log2(math.e)


def grid_shape(count):
    rows = max(d for d in range(1, math.isqrt(count) + 1) if count % d == 0)
    return rows, count // rows


def neighbour_of(region, shift, across, shape):
    rows, cols = shape
    y, x = region // cols, region % cols
    if across:
        return y * cols + (x + shift) % cols
    return ((y + shift) % rows) * cols + x


def pairs_of(count, shift, across, shape):
    return [(neighbour_of(d, shift, across, shape), d) for d in range(count)]


def reversed_pairs(pairs):
    return [(d, s) for s, d in pairs]


def padded(n):
    return -(-n // TILE_ROWS) * TILE_ROWS


class Chunk:
    def __init__(self, first, heads, across, visit_at):
        self.first, self.heads, self.across, self.visit_at = first, heads, across, visit_at

    def sizes(self, shape):
        rows, cols = shape
        return (rows, cols) if self.across else (cols, rows)

    def message_rows(self, rows):
        return self.heads * rows + padded(3 * self.heads)


def gather_kernel(moves, *refs):
    n_outs = 1 + max(m[2] for m in moves)
    sources, outs, sems = refs[: -1 - n_outs], refs[-1 - n_outs : -1], refs[-1]
    copies = []
    for i, (source, start, target, layer, at, width) in enumerate(moves):
        to = outs[target] if layer is None else outs[target].at[layer]
        copies.append(
            pltpu.make_async_copy(
                sources[source].at[:, start : start + width],
                to.at[:, at : at + width],
                sems.at[i],
            )
        )
    for copy in copies:
        copy.start()
    for copy in copies:
        copy.wait()


def block_rule(chunk, count, shape, v, s, stale):
    ids = [
        (neighbour_of(d, v, not chunk.across, shape), neighbour_of(d, s, chunk.across, shape))
        for d in range(count)
    ]
    if stale:
        return False if all(q == m for q, m in ids) else True
    close = [abs(q - m) <= 1 for q, m in ids]
    if all(close):
        return None
    return [d for d in range(count) if close[d]] if any(close) else False


def blocks_of(chunks, count, shape):
    entries, rules = [], []
    for chunk in chunks:
        n_visit, n_share = chunk.sizes(shape)
        per_chunk = []
        for v in range(n_visit):
            per_visit = []
            for s in range(n_share):
                for stale in (0, 1):
                    rule = block_rule(chunk, count, shape, v, s, stale)
                    if rule is False:
                        continue
                    key = (chunk.across, v, s, stale, rule)
                    if rule is not None and key not in rules:
                        rules.append(key)
                    per_visit.append((s, stale, None if rule is None else rules.index(key)))
            per_chunk.append(per_visit)
        entries.append(per_chunk)
    return entries, rules


def table_kernel(rules, shape, listed, out):
    region = lax.axis_index("reg")
    for i, (across, v, s, stale, rule) in enumerate(rules):
        if stale:
            query_region = neighbour_of(region, v, not across, shape)
            key_region = neighbour_of(region, s, across, shape)
            hit = listed[query_region, 0] == key_region
            for j in range(1, listed.shape[1]):
                hit = hit | (listed[query_region, j] == key_region)
        else:
            hit = functools.reduce(jnp.logical_or, [region == d for d in rule])
        bias = jnp.where(hit, 0.0, NEVER).astype(jnp.float32)
        out[i : i + 1, :] = jnp.full((1, LANES), bias, jnp.float32)


def attend_kernel(chunks, blocks, sizes, rows, *refs):
    refs = list(refs)
    table = refs.pop(0)
    local = {}
    for chunk, (n_visit, n_share) in zip(chunks, sizes):
        local[chunk] = (
            [refs.pop(0) for _ in range(n_visit)],
            [refs.pop(0) for _ in range(n_share)],
        )
    outs = {}
    for chunk, (n_visit, _) in zip(chunks, sizes):
        outs[chunk] = (refs.pop(0), refs.pop(0), [refs.pop(0) for _ in range(n_visit - 1)])
    lane = lax.broadcasted_iota(jnp.int32, (rows, LANES), 1)
    for chunk, plan, (n_visit, n_share) in zip(chunks, blocks, sizes):
        queries, shared = local[chunk]
        out_own, lse_own, messages = outs[chunk]
        heads = chunk.heads
        lse_all = [jnp.zeros((rows, LANES), jnp.float32) for _ in range(n_visit)]
        for h in range(heads):
            there = slice(h * HD, (h + 1) * HD)
            visiting = slice((chunk.visit_at + h) * HD, (chunk.visit_at + h + 1) * HD)
            for v in range(n_visit):
                q = queries[v][:, visiting]
                keys = jnp.concatenate([shared[s][2 * t, :, there] for s, t, _ in plan[v]], axis=0)
                values = jnp.concatenate(
                    [shared[s][2 * t + 1, :, there] for s, t, _ in plan[v]], axis=0
                )
                values = jnp.concatenate(
                    [values, jnp.ones((values.shape[0], LANES), jnp.bfloat16)], axis=1
                )
                scores = lax.dot_general(
                    q, keys, (((1,), (1,)), ((), ())), preferred_element_type=jnp.float32
                )
                pieces = []
                for i, (_, _, line) in enumerate(plan[v]):
                    piece = scores[:, i * rows : (i + 1) * rows]
                    pieces.append(piece if line is None else piece + table[line : line + 1, :])
                peak = functools.reduce(jnp.maximum, pieces).max(axis=1, keepdims=True) * SCALE2
                weights = [jnp.exp2(p * SCALE2 - peak).astype(jnp.bfloat16) for p in pieces]
                both = jnp.dot(
                    jnp.concatenate(weights, axis=1), values, preferred_element_type=jnp.float32
                )
                total = both[:, HD:]
                out = (both[:, :HD] / total).astype(jnp.bfloat16)
                lse_all[v] = jnp.where(lane == h, peak + jnp.log2(total), lse_all[v])
                if v == 0:
                    out_own[:, there] = out
                else:
                    messages[v - 1][h * rows : (h + 1) * rows, :] = out
        lse_own[...] = lse_all[0].T[: padded(heads)]
        for v in range(1, n_visit):
            flat = lse_all[v].T[: padded(heads)]
            high = flat.astype(jnp.bfloat16).astype(jnp.float32)
            middle = (flat - high).astype(jnp.bfloat16).astype(jnp.float32)
            low = flat - high - middle
            lines = [x[:heads] for x in (high, middle, low)]
            spare = padded(3 * heads) - 3 * heads
            if spare:
                lines.append(jnp.zeros((spare, rows), jnp.float32))
            messages[v - 1][heads * rows :, :] = jnp.concatenate(lines, axis=0).astype(jnp.bfloat16)


def merge_into(chunks, n_visits, rows, refs, buffer):
    first = min(c.first for c in chunks)
    at = 0
    for chunk, n_visit in zip(chunks, n_visits):
        heads = chunk.heads
        part, lse_own = refs[at], refs[at + 1]
        messages = refs[at + 2 : at + 1 + n_visit]
        at += 1 + n_visit
        flats = [lse_own[:heads]]
        for message in messages:
            lines = message[heads * rows :, :].astype(jnp.float32)
            flats.append(
                lines[:heads] + lines[heads : 2 * heads] + lines[2 * heads : 3 * heads]
            )
        top = functools.reduce(jnp.maximum, flats)
        weights = [jnp.exp2(f - top) for f in flats]
        denom = functools.reduce(jnp.add, weights)
        blank = jnp.zeros((LANES - heads, rows), jnp.float32)
        columns = [jnp.concatenate([w / denom, blank], axis=0).T for w in weights]
        for h in range(heads):
            cols = slice(h * HD, (h + 1) * HD)
            parts = [part[:, cols]] + [m[h * rows : (h + 1) * rows, :] for m in messages]
            value = functools.reduce(
                jnp.add,
                [c[:, h : h + 1] * p.astype(jnp.float32) for c, p in zip(columns, parts)],
            )
            to = chunk.first - first + h
            buffer[:, to * HD : (to + 1) * HD] = value.astype(jnp.bfloat16)


def early_merge_kernel(chunks, n_visits, rows, *refs):
    merge_into(chunks, n_visits, rows, refs[:-1], refs[-1])


def last_merge_kernel(chunks, n_visits, rows, starts, *refs):
    out, buffer, sems = refs[-3:]
    done = refs[: len(starts)]
    copies = [
        pltpu.make_async_copy(ref, out.at[:, at : at + ref.shape[1]], sems.at[i])
        for i, (ref, at) in enumerate(zip(done, starts))
    ]
    for copy in copies:
        copy.start()
    merge_into(chunks, n_visits, rows, refs[len(starts) : -3], buffer)
    first = min(c.first for c in chunks) * HD
    copies.append(
        pltpu.make_async_copy(
            buffer, out.at[:, first : first + buffer.shape[1]], sems.at[len(starts)]
        )
    )
    copies[-1].start()
    for copy in copies:
        copy.wait()


def plan_of(heads):
    half = heads // 2
    later = max(1, half // 3)
    early = half - later
    stages = []
    at = 0
    for n, visit_at in ((early, 0), (later, early)):
        if n:
            stages.append([Chunk(at, n, True, visit_at), Chunk(at + n, n, False, visit_at)])
            at += 2 * n
    return stages


def placement(resident):
    if resident:
        return (
            lambda x: pltpu.with_memory_space_constraint(x, pltpu.VMEM),
            lambda shape, dtype: pltpu.VMEM(shape, dtype),
        )
    return lambda x: x, jax.ShapeDtypeStruct


def on_device(count, queries, keys_now, values_now, keys_stale, values_stale, neighbours):
    rows, width = queries.shape
    assert rows == LANES
    shape = grid_shape(count)
    stages = plan_of(width // HD)
    chunks = [c for stage in stages for c in stage]
    assert sum(c.heads for c in chunks) * HD == width
    arriving = sum((c.sizes(shape)[1] - 1) * 4 * rows * c.heads * HD * 2 for c in chunks)
    resident = arriving <= VMEM_BUDGET
    in_vmem, result = placement(resident)
    params = pltpu.CompilerParams(vmem_limit_bytes=KERNEL_VMEM if resident else None)
    vmem = pl.BlockSpec(memory_space=pltpu.VMEM)
    in_hbm = pl.BlockSpec(memory_space=pltpu.HBM)

    def gather(moves, sources, shapes):
        return pl.pallas_call(
            functools.partial(gather_kernel, moves),
            in_specs=[in_hbm] * len(sources),
            out_specs=[vmem] * len(shapes),
            out_shape=[result(x, jnp.bfloat16) for x in shapes],
            scratch_shapes=[pltpu.SemaphoreType.DMA((len(moves),))],
            compiler_params=params,
            name="gather",
        )(*[pltpu.with_memory_space_constraint(x, pltpu.HBM) for x in sources])

    by_way = {way: [c for c in chunks if c.across == way] for way in (True, False)}
    moves = [
        (0, c.first * HD, int(way), None, c.visit_at * HD, c.heads * HD)
        for way in (True, False)
        for c in by_way[way]
    ]
    widths = [sum(c.heads for c in by_way[bool(i)]) * HD for i in range(2)]
    mine = gather(moves, [queries], [(rows, w) for w in widths])
    visiting = {
        way: [mine[int(way)]]
        + [
            lax.ppermute(mine[int(way)], "reg", pairs_of(count, v, not way, shape))
            for v in range(1, by_way[way][0].sizes(shape)[0])
        ]
        for way in (True, False)
    }
    moves = [
        (a, c.first * HD, i, a, 0, c.heads * HD) for i, c in enumerate(chunks) for a in range(4)
    ]
    packed = gather(
        moves,
        [keys_now, values_now, keys_stale, values_stale],
        [(4, rows, c.heads * HD) for c in chunks],
    )
    shared = {
        chunk: [pack]
        + [
            lax.ppermute(pack, "reg", pairs_of(count, s, chunk.across, shape))
            for s in range(1, chunk.sizes(shape)[1])
        ]
        for chunk, pack in zip(chunks, packed)
    }

    blocks, rules = blocks_of(chunks, count, shape)
    blocks = dict(zip(chunks, blocks))
    table = pl.pallas_call(
        functools.partial(table_kernel, rules, shape),
        in_specs=[pl.BlockSpec(memory_space=pltpu.SMEM)],
        out_specs=vmem,
        out_shape=result((padded(len(rules)), LANES), jnp.float32),
        compiler_params=params,
            name="table",
    )(neighbours)

    results = {}
    for stage in stages:
        sizes = [c.sizes(shape) for c in stage]
        operands = [table]
        for chunk in stage:
            operands += visiting[chunk.across] + shared[chunk]
        out_shape = []
        for chunk, (n_visit, _) in zip(stage, sizes):
            out_shape += [
                result((rows, chunk.heads * HD), jnp.bfloat16),
                result((padded(chunk.heads), rows), jnp.float32),
            ]
            out_shape += [result((chunk.message_rows(rows), HD), jnp.bfloat16)] * (n_visit - 1)
        outs = pl.pallas_call(
            functools.partial(attend_kernel, stage, [blocks[c] for c in stage], sizes, rows),
            in_specs=[vmem] * len(operands),
            out_specs=[vmem] * len(out_shape),
            out_shape=out_shape,
            compiler_params=params,
            name="attend",
        )(*[in_vmem(x) for x in operands])
        outs = list(outs)
        for chunk, (n_visit, _) in zip(stage, sizes):
            kept = [outs.pop(0), outs.pop(0)]
            for v in range(1, n_visit):
                pairs = reversed_pairs(pairs_of(count, v, not chunk.across, shape))
                kept.append(lax.ppermute(outs.pop(0), "reg", pairs))
            results[chunk] = [in_vmem(x) for x in kept]

    merged, starts = [], []
    for stage in stages[:-1]:
        operands = [x for c in stage for x in results[c]]
        merged.append(
            pl.pallas_call(
                functools.partial(
                    early_merge_kernel, stage, [c.sizes(shape)[0] for c in stage], rows
                ),
                in_specs=[vmem] * len(operands),
                out_specs=vmem,
                out_shape=result((rows, sum(c.heads for c in stage) * HD), jnp.bfloat16),
                compiler_params=params,
            name="merge",
            )(*operands)
        )
        starts.append(min(c.first for c in stage) * HD)
    stage = stages[-1]
    operands = [x for c in stage for x in results[c]]
    return pl.pallas_call(
        functools.partial(
            last_merge_kernel, stage, [c.sizes(shape)[0] for c in stage], rows, starts
        ),
        in_specs=[vmem] * (len(merged) + len(operands)),
        out_specs=in_hbm,
        out_shape=jax.ShapeDtypeStruct((rows, width), jnp.bfloat16),
        scratch_shapes=[
            pltpu.VMEM((rows, sum(c.heads for c in stage) * HD), jnp.bfloat16),
            pltpu.SemaphoreType.DMA((len(stages),)),
        ],
        compiler_params=params,
            name="finish",
    )(*[in_vmem(x) for x in merged], *operands)


def solution(mesh):
    in_specs = (
        P(("grp", "reg"), None),
        P(("grp", "reg"), None),
        P(("grp", "reg"), None),
        P(("grp", "reg"), None),
        P(("grp", "reg"), None),
        P("grp", None),
    )
    out_specs = P(("grp", "reg"), None)
    return jax.shard_map(
        functools.partial(on_device, mesh.shape["reg"]),
        mesh=mesh,
        in_specs=in_specs,
        out_specs=out_specs,
        check_vma=False,
    )
```

```python
import functools
import math

import jax
import jax.numpy as jnp
from jax import lax
from jax.experimental import pallas as pl
from jax.experimental.pallas import tpu as pltpu
from jax.sharding import PartitionSpec as P


HD = 128
LANES = 128
TILE_ROWS = 16
NEVER = -1e30
VMEM_BUDGET = 2 << 20
N_CHUNKS = 4
KERNEL_VMEM = 2 << 20
SCALE2 = HD**-0.5 * math.log2(math.e)


def grid_shape(count):
    rows = max(d for d in range(1, math.isqrt(count) + 1) if count % d == 0)
    return rows, count // rows


def neighbour_of(region, shift, across, shape):
    rows, cols = shape
    y, x = region // cols, region % cols
    if across:
        return y * cols + (x + shift) % cols
    return ((y + shift) % rows) * cols + x


def pairs_of(count, shift, across, shape):
    return [(neighbour_of(d, shift, across, shape), d) for d in range(count)]


def reversed_pairs(pairs):
    return [(d, s) for s, d in pairs]


def padded(n):
    return -(-n // TILE_ROWS) * TILE_ROWS


class Chunk:
    def __init__(self, first, heads, across, visit_at):
        self.first, self.heads, self.across, self.visit_at = first, heads, across, visit_at

    def sizes(self, shape):
        rows, cols = shape
        return (rows, cols) if self.across else (cols, rows)

    def message_rows(self, rows):
        return self.heads * rows + padded(3 * self.heads)


def gather_kernel(moves, n_after, *refs):
    refs = refs[n_after:]
    n_outs = 1 + max(m[2] for m in moves)
    sources, outs, sems = refs[: -1 - n_outs], refs[-1 - n_outs : -1], refs[-1]
    copies = []
    for i, (source, start, target, layer, at, width) in enumerate(moves):
        to = outs[target] if layer is None else outs[target].at[layer]
        copies.append(
            pltpu.make_async_copy(
                sources[source].at[:, start : start + width],
                to.at[:, at : at + width],
                sems.at[i],
            )
        )
    for copy in copies:
        copy.start()
    for copy in copies:
        copy.wait()


def block_rule(chunk, count, shape, v, s, stale):
    ids = [
        (neighbour_of(d, v, not chunk.across, shape), neighbour_of(d, s, chunk.across, shape))
        for d in range(count)
    ]
    if stale:
        return False if all(q == m for q, m in ids) else True
    close = [abs(q - m) <= 1 for q, m in ids]
    if all(close):
        return None
    return [d for d in range(count) if close[d]] if any(close) else False


def blocks_of(chunks, count, shape):
    entries, rules = [], []
    for chunk in chunks:
        n_visit, n_share = chunk.sizes(shape)
        per_chunk = []
        for v in range(n_visit):
            per_visit = []
            for s in range(n_share):
                for stale in (0, 1):
                    rule = block_rule(chunk, count, shape, v, s, stale)
                    if rule is False:
                        continue
                    key = (chunk.across, v, s, stale, rule)
                    if rule is not None and key not in rules:
                        rules.append(key)
                    per_visit.append((s, stale, None if rule is None else rules.index(key)))
            per_chunk.append(per_visit)
        entries.append(per_chunk)
    return entries, rules


def table_kernel(rules, shape, listed, out):
    region = lax.axis_index("reg")
    for i, (across, v, s, stale, rule) in enumerate(rules):
        if stale:
            query_region = neighbour_of(region, v, not across, shape)
            key_region = neighbour_of(region, s, across, shape)
            hit = listed[0, query_region] == key_region
            for j in range(1, listed.shape[0]):
                hit = hit | (listed[j, query_region] == key_region)
        else:
            hit = functools.reduce(jnp.logical_or, [region == d for d in rule])
        bias = jnp.where(hit, 0.0, NEVER).astype(jnp.float32)
        out[i : i + 1, :] = jnp.full((1, LANES), bias, jnp.float32)


def attend_kernel(chunks, blocks, sizes, rows, *refs):
    refs = list(refs)
    table = refs.pop(0)
    local = {}
    for chunk, (n_visit, n_share) in zip(chunks, sizes):
        local[chunk] = (
            [refs.pop(0) for _ in range(n_visit)],
            [refs.pop(0) for _ in range(n_share)],
        )
    outs = {}
    for chunk, (n_visit, _) in zip(chunks, sizes):
        outs[chunk] = (refs.pop(0), refs.pop(0), [refs.pop(0) for _ in range(n_visit - 1)])
    lane = lax.broadcasted_iota(jnp.int32, (rows, LANES), 1)
    for chunk, plan, (n_visit, n_share) in zip(chunks, blocks, sizes):
        queries, shared = local[chunk]
        out_own, lse_own, messages = outs[chunk]
        heads = chunk.heads
        lse_all = [jnp.zeros((rows, LANES), jnp.float32) for _ in range(n_visit)]
        for h in range(heads):
            there = slice(h * HD, (h + 1) * HD)
            visiting = slice((chunk.visit_at + h) * HD, (chunk.visit_at + h + 1) * HD)
            for v in range(n_visit):
                q = queries[v][:, visiting]
                keys = jnp.concatenate([shared[s][2 * t, :, there] for s, t, _ in plan[v]], axis=0)
                values = jnp.concatenate(
                    [shared[s][2 * t + 1, :, there] for s, t, _ in plan[v]], axis=0
                )
                values = jnp.concatenate(
                    [values, jnp.ones((values.shape[0], LANES), jnp.bfloat16)], axis=1
                )
                scores = lax.dot_general(
                    q, keys, (((1,), (1,)), ((), ())), preferred_element_type=jnp.float32
                )
                pieces = []
                for i, (_, _, line) in enumerate(plan[v]):
                    piece = scores[:, i * rows : (i + 1) * rows]
                    pieces.append(piece if line is None else piece + table[line : line + 1, :])
                peak = functools.reduce(jnp.maximum, pieces).max(axis=1, keepdims=True) * SCALE2
                weights = [jnp.exp2(p * SCALE2 - peak).astype(jnp.bfloat16) for p in pieces]
                both = jnp.dot(
                    jnp.concatenate(weights, axis=1), values, preferred_element_type=jnp.float32
                )
                total = both[:, HD:]
                out = (both[:, :HD] / total).astype(jnp.bfloat16)
                lse_all[v] = jnp.where(lane == h, peak + jnp.log2(total), lse_all[v])
                if v == 0:
                    out_own[:, there] = out
                else:
                    messages[v - 1][h * rows : (h + 1) * rows, :] = out
        lse_own[...] = lse_all[0].T[: padded(heads)]
        for v in range(1, n_visit):
            flat = lse_all[v].T[: padded(heads)]
            high = flat.astype(jnp.bfloat16).astype(jnp.float32)
            middle = (flat - high).astype(jnp.bfloat16).astype(jnp.float32)
            low = flat - high - middle
            lines = [x[:heads] for x in (high, middle, low)]
            spare = padded(3 * heads) - 3 * heads
            if spare:
                lines.append(jnp.zeros((spare, rows), jnp.float32))
            messages[v - 1][heads * rows :, :] = jnp.concatenate(lines, axis=0).astype(jnp.bfloat16)


def merge_into(chunks, n_visits, rows, refs, buffer):
    first = min(c.first for c in chunks)
    at = 0
    for chunk, n_visit in zip(chunks, n_visits):
        heads = chunk.heads
        part, lse_own = refs[at], refs[at + 1]
        messages = refs[at + 2 : at + 1 + n_visit]
        at += 1 + n_visit
        flats = [lse_own[:heads]]
        for message in messages:
            lines = message[heads * rows :, :].astype(jnp.float32)
            flats.append(
                lines[:heads] + lines[heads : 2 * heads] + lines[2 * heads : 3 * heads]
            )
        top = functools.reduce(jnp.maximum, flats)
        weights = [jnp.exp2(f - top) for f in flats]
        denom = functools.reduce(jnp.add, weights)
        blank = jnp.zeros((LANES - heads, rows), jnp.float32)
        columns = [jnp.concatenate([w / denom, blank], axis=0).T for w in weights]
        for h in range(heads):
            cols = slice(h * HD, (h + 1) * HD)
            parts = [part[:, cols]] + [m[h * rows : (h + 1) * rows, :] for m in messages]
            value = functools.reduce(
                jnp.add,
                [c[:, h : h + 1] * p.astype(jnp.float32) for c, p in zip(columns, parts)],
            )
            to = chunk.first - first + h
            buffer[:, to * HD : (to + 1) * HD] = value.astype(jnp.bfloat16)


def early_merge_kernel(chunks, n_visits, rows, *refs):
    merge_into(chunks, n_visits, rows, refs[:-1], refs[-1])


def last_merge_kernel(chunks, n_visits, rows, starts, *refs):
    out, buffer, sems = refs[-3:]
    done = refs[: len(starts)]
    copies = [
        pltpu.make_async_copy(ref, out.at[:, at : at + ref.shape[1]], sems.at[i])
        for i, (ref, at) in enumerate(zip(done, starts))
    ]
    for copy in copies:
        copy.start()
    merge_into(chunks, n_visits, rows, refs[len(starts) : -3], buffer)
    first = min(c.first for c in chunks) * HD
    copies.append(
        pltpu.make_async_copy(
            buffer, out.at[:, first : first + buffer.shape[1]], sems.at[len(starts)]
        )
    )
    copies[-1].start()
    for copy in copies:
        copy.wait()


def plan_of(heads):
    half = heads // 2
    later = max(1, half // 3)
    early = half - later
    stages = []
    at = 0
    for n, visit_at in ((early, 0), (later, early)):
        if n:
            stages.append([Chunk(at, n, True, visit_at), Chunk(at + n, n, False, visit_at)])
            at += 2 * n
    return stages


def placement(resident):
    if resident:
        return (
            lambda x: pltpu.with_memory_space_constraint(x, pltpu.VMEM),
            lambda shape, dtype: pltpu.VMEM(shape, dtype),
        )
    return lambda x: x, jax.ShapeDtypeStruct


def on_device(count, queries, keys_now, values_now, keys_stale, values_stale, neighbours):
    rows, width = queries.shape
    assert rows == LANES
    shape = grid_shape(count)
    stages = plan_of(width // HD)
    chunks = [c for stage in stages for c in stage]
    assert sum(c.heads for c in chunks) * HD == width and len(chunks) == N_CHUNKS
    arriving = sum((c.sizes(shape)[1] - 1) * 4 * rows * c.heads * HD * 2 for c in chunks)
    resident = arriving <= VMEM_BUDGET
    in_vmem, result = placement(resident)
    params = pltpu.CompilerParams(vmem_limit_bytes=KERNEL_VMEM if resident else None)
    vmem = pl.BlockSpec(memory_space=pltpu.VMEM)
    in_hbm = pl.BlockSpec(memory_space=pltpu.HBM)

    def gather(moves, sources, shapes, after=()):
        return pl.pallas_call(
            functools.partial(gather_kernel, moves, len(after)),
            in_specs=[vmem if resident else in_hbm] * len(after) + [in_hbm] * len(sources),
            out_specs=[vmem] * len(shapes),
            out_shape=[result(x, jnp.bfloat16) for x in shapes],
            scratch_shapes=[pltpu.SemaphoreType.DMA((len(moves),))],
            compiler_params=params,
            name="gather",
        )(
            *[in_vmem(x) for x in after],
            *[pltpu.with_memory_space_constraint(x, pltpu.HBM) for x in sources],
        )

    by_way = {way: [c for c in chunks if c.across == way] for way in (True, False)}
    moves = [
        (0, c.first * HD, int(way), None, c.visit_at * HD, c.heads * HD)
        for way in (True, False)
        for c in by_way[way]
    ]
    widths = [sum(c.heads for c in by_way[bool(i)]) * HD for i in range(2)]
    mine = gather(moves, [queries], [(rows, w) for w in widths])
    visiting = {}
    for way in (False, True):
        visiting[way] = [mine[int(way)]] + [
            lax.ppermute(mine[int(way)], "reg", pairs_of(count, v, not way, shape))
            for v in range(1, by_way[way][0].sizes(shape)[0])
        ]
    moves = [
        (a, c.first * HD, i, a, 0, c.heads * HD) for i, c in enumerate(chunks) for a in range(4)
    ]
    packed = gather(
        moves,
        [keys_now, values_now, keys_stale, values_stale],
        [(4, rows, c.heads * HD) for c in chunks],
        after=mine,
    )
    shared = {}
    for chunk, pack in zip(chunks, packed):
        shared[chunk] = [pack] + [
            lax.ppermute(pack, "reg", pairs_of(count, s, chunk.across, shape))
            for s in range(1, chunk.sizes(shape)[1])
        ]

    blocks, rules = blocks_of(chunks, count, shape)
    blocks = dict(zip(chunks, blocks))
    table = pl.pallas_call(
        functools.partial(table_kernel, rules, shape),
        in_specs=[pl.BlockSpec(memory_space=pltpu.SMEM)],
        out_specs=vmem,
        out_shape=result((padded(len(rules)), LANES), jnp.float32),
        compiler_params=params,
            name="table",
    )(neighbours.T)

    results = {}
    for stage in [[c] for c in chunks]:
        sizes = [c.sizes(shape) for c in stage]
        operands = [table]
        for chunk in stage:
            operands += visiting[chunk.across] + shared[chunk]
        out_shape = []
        for chunk, (n_visit, _) in zip(stage, sizes):
            out_shape += [
                result((rows, chunk.heads * HD), jnp.bfloat16),
                result((padded(chunk.heads), rows), jnp.float32),
            ]
            out_shape += [result((chunk.message_rows(rows), HD), jnp.bfloat16)] * (n_visit - 1)
        outs = pl.pallas_call(
            functools.partial(attend_kernel, stage, [blocks[c] for c in stage], sizes, rows),
            in_specs=[vmem] * len(operands),
            out_specs=[vmem] * len(out_shape),
            out_shape=out_shape,
            compiler_params=params,
            name="attend",
        )(*[in_vmem(x) for x in operands])
        outs = list(outs)
        for chunk, (n_visit, _) in zip(stage, sizes):
            kept = [outs.pop(0), outs.pop(0)]
            for v in range(1, n_visit):
                pairs = reversed_pairs(pairs_of(count, v, not chunk.across, shape))
                kept.append(lax.ppermute(outs.pop(0), "reg", pairs))
            results[chunk] = [in_vmem(x) for x in kept]

    merged, starts = [], []
    for stage in stages[:-1]:
        operands = [x for c in stage for x in results[c]]
        merged.append(
            pl.pallas_call(
                functools.partial(
                    early_merge_kernel, stage, [c.sizes(shape)[0] for c in stage], rows
                ),
                in_specs=[vmem] * len(operands),
                out_specs=vmem,
                out_shape=result((rows, sum(c.heads for c in stage) * HD), jnp.bfloat16),
                compiler_params=params,
            name="merge",
            )(*operands)
        )
        starts.append(min(c.first for c in stage) * HD)
    stage = stages[-1]
    operands = [x for c in stage for x in results[c]]
    return pl.pallas_call(
        functools.partial(
            last_merge_kernel, stage, [c.sizes(shape)[0] for c in stage], rows, starts
        ),
        in_specs=[vmem] * (len(merged) + len(operands)),
        out_specs=in_hbm,
        out_shape=jax.ShapeDtypeStruct((rows, width), jnp.bfloat16),
        scratch_shapes=[
            pltpu.VMEM((rows, sum(c.heads for c in stage) * HD), jnp.bfloat16),
            pltpu.SemaphoreType.DMA((len(stages),)),
        ],
        compiler_params=params,
            name="finish",
    )(*[in_vmem(x) for x in merged], *operands)


def solution(mesh):
    in_specs = (
        P(("grp", "reg"), None),
        P(("grp", "reg"), None),
        P(("grp", "reg"), None),
        P(("grp", "reg"), None),
        P(("grp", "reg"), None),
        P("grp", None),
    )
    out_specs = P(("grp", "reg"), None)

    def step(*args):
        return on_device(mesh.shape["reg"], *args)

    return jax.shard_map(
        step, mesh=mesh, in_specs=in_specs, out_specs=out_specs, check_vma=False
    )
```

```python
import functools
import math

import jax
import jax.numpy as jnp
from jax import lax
from jax.experimental import pallas as pl
from jax.experimental.pallas import tpu as pltpu
from jax.sharding import PartitionSpec as P


HD = 128
LANES = 128
TILE_ROWS = 16
NEVER = -1e30
VMEM_BUDGET = 2 << 20
KERNEL_VMEM = 2 << 20
SCALE2 = HD**-0.5 * math.log2(math.e)


def grid_shape(count):
    rows = max(d for d in range(1, math.isqrt(count) + 1) if count % d == 0)
    return rows, count // rows


def neighbour_of(region, shift, across, shape):
    rows, cols = shape
    y, x = region // cols, region % cols
    if across:
        return y * cols + (x + shift) % cols
    return ((y + shift) % rows) * cols + x


def pairs_of(count, shift, across, shape):
    return [(neighbour_of(d, shift, across, shape), d) for d in range(count)]


def reversed_pairs(pairs):
    return [(d, s) for s, d in pairs]


def padded(n):
    return -(-n // TILE_ROWS) * TILE_ROWS


class Chunk:
    def __init__(self, first, heads, across, visit_at):
        self.first, self.heads, self.across, self.visit_at = first, heads, across, visit_at

    def sizes(self, shape):
        rows, cols = shape
        return (rows, cols) if self.across else (cols, rows)

    def message_rows(self, rows):
        return self.heads * rows + padded(3 * self.heads)


def gather_kernel(moves, n_after, *refs):
    refs = refs[n_after:]
    n_outs = 1 + max(m[2] for m in moves)
    sources, outs, sems = refs[: -1 - n_outs], refs[-1 - n_outs : -1], refs[-1]
    copies = []
    for i, (source, start, target, layer, at, width) in enumerate(moves):
        to = outs[target] if layer is None else outs[target].at[layer]
        copies.append(
            pltpu.make_async_copy(
                sources[source].at[:, start : start + width],
                to.at[:, at : at + width],
                sems.at[i],
            )
        )
    for copy in copies:
        copy.start()
    for copy in copies:
        copy.wait()


def block_rule(chunk, count, shape, v, s, stale):
    ids = [
        (neighbour_of(d, v, not chunk.across, shape), neighbour_of(d, s, chunk.across, shape))
        for d in range(count)
    ]
    if stale:
        return False if all(q == m for q, m in ids) else True
    close = [abs(q - m) <= 1 for q, m in ids]
    if all(close):
        return None
    return [d for d in range(count) if close[d]] if any(close) else False


def blocks_of(chunks, count, shape):
    entries, rules = [], []
    for chunk in chunks:
        n_visit, n_share = chunk.sizes(shape)
        per_chunk = []
        for v in range(n_visit):
            per_visit = []
            for s in range(n_share):
                for stale in (0, 1):
                    rule = block_rule(chunk, count, shape, v, s, stale)
                    if rule is False:
                        continue
                    key = (chunk.across, v, s, stale, rule)
                    if rule is not None and key not in rules:
                        rules.append(key)
                    per_visit.append((s, stale, None if rule is None else rules.index(key)))
            per_chunk.append(per_visit)
        entries.append(per_chunk)
    return entries, rules


def table_kernel(rules, shape, listed, out):
    region = lax.axis_index("reg")
    for i, (across, v, s, stale, rule) in enumerate(rules):
        if stale:
            query_region = neighbour_of(region, v, not across, shape)
            key_region = neighbour_of(region, s, across, shape)
            hit = listed[0, query_region] == key_region
            for j in range(1, listed.shape[0]):
                hit = hit | (listed[j, query_region] == key_region)
        else:
            hit = functools.reduce(jnp.logical_or, [region == d for d in rule])
        bias = jnp.where(hit, 0.0, NEVER).astype(jnp.float32)
        out[i : i + 1, :] = jnp.full((1, LANES), bias, jnp.float32)


def attend_kernel(chunks, blocks, sizes, rows, *refs):
    refs = list(refs)
    table = refs.pop(0)
    local = {}
    for chunk, (n_visit, n_share) in zip(chunks, sizes):
        local[chunk] = (
            [refs.pop(0) for _ in range(n_visit)],
            [refs.pop(0) for _ in range(n_share)],
        )
    outs = {}
    for chunk, (n_visit, _) in zip(chunks, sizes):
        outs[chunk] = (refs.pop(0), refs.pop(0), [refs.pop(0) for _ in range(n_visit - 1)])
    lane = lax.broadcasted_iota(jnp.int32, (rows, LANES), 1)
    for chunk, plan, (n_visit, n_share) in zip(chunks, blocks, sizes):
        queries, shared = local[chunk]
        out_own, lse_own, messages = outs[chunk]
        heads = chunk.heads
        lse_all = [jnp.zeros((rows, LANES), jnp.float32) for _ in range(n_visit)]
        for h in range(heads):
            there = slice(h * HD, (h + 1) * HD)
            visiting = slice((chunk.visit_at + h) * HD, (chunk.visit_at + h + 1) * HD)
            for v in range(n_visit):
                q = queries[v][:, visiting]
                keys = jnp.concatenate([shared[s][2 * t, :, there] for s, t, _ in plan[v]], axis=0)
                values = jnp.concatenate(
                    [shared[s][2 * t + 1, :, there] for s, t, _ in plan[v]], axis=0
                )
                values = jnp.concatenate(
                    [values, jnp.ones((values.shape[0], LANES), jnp.bfloat16)], axis=1
                )
                scores = lax.dot_general(
                    q, keys, (((1,), (1,)), ((), ())), preferred_element_type=jnp.float32
                )
                pieces = []
                for i, (_, _, line) in enumerate(plan[v]):
                    piece = scores[:, i * rows : (i + 1) * rows]
                    pieces.append(piece if line is None else piece + table[line : line + 1, :])
                peak = functools.reduce(jnp.maximum, pieces).max(axis=1, keepdims=True) * SCALE2
                weights = [jnp.exp2(p * SCALE2 - peak).astype(jnp.bfloat16) for p in pieces]
                both = jnp.dot(
                    jnp.concatenate(weights, axis=1), values, preferred_element_type=jnp.float32
                )
                total = both[:, HD:]
                out = (both[:, :HD] / total).astype(jnp.bfloat16)
                lse_all[v] = jnp.where(lane == h, peak + jnp.log2(total), lse_all[v])
                if v == 0:
                    out_own[:, there] = out
                else:
                    messages[v - 1][h * rows : (h + 1) * rows, :] = out
        lse_own[...] = lse_all[0].T[: padded(heads)]
        for v in range(1, n_visit):
            flat = lse_all[v].T[: padded(heads)]
            high = flat.astype(jnp.bfloat16).astype(jnp.float32)
            middle = (flat - high).astype(jnp.bfloat16).astype(jnp.float32)
            low = flat - high - middle
            lines = [x[:heads] for x in (high, middle, low)]
            spare = padded(3 * heads) - 3 * heads
            if spare:
                lines.append(jnp.zeros((spare, rows), jnp.float32))
            messages[v - 1][heads * rows :, :] = jnp.concatenate(lines, axis=0).astype(jnp.bfloat16)


def merge_into(chunks, n_visits, rows, refs, buffer):
    first = min(c.first for c in chunks)
    at = 0
    for chunk, n_visit in zip(chunks, n_visits):
        heads = chunk.heads
        part, lse_own = refs[at], refs[at + 1]
        messages = refs[at + 2 : at + 1 + n_visit]
        at += 1 + n_visit
        flats = [lse_own[:heads]]
        for message in messages:
            lines = message[heads * rows :, :].astype(jnp.float32)
            flats.append(
                lines[:heads] + lines[heads : 2 * heads] + lines[2 * heads : 3 * heads]
            )
        top = functools.reduce(jnp.maximum, flats)
        weights = [jnp.exp2(f - top) for f in flats]
        denom = functools.reduce(jnp.add, weights)
        blank = jnp.zeros((LANES - heads, rows), jnp.float32)
        columns = [jnp.concatenate([w / denom, blank], axis=0).T for w in weights]
        for h in range(heads):
            cols = slice(h * HD, (h + 1) * HD)
            parts = [part[:, cols]] + [m[h * rows : (h + 1) * rows, :] for m in messages]
            value = functools.reduce(
                jnp.add,
                [c[:, h : h + 1] * p.astype(jnp.float32) for c, p in zip(columns, parts)],
            )
            to = chunk.first - first + h
            buffer[:, to * HD : (to + 1) * HD] = value.astype(jnp.bfloat16)


def early_merge_kernel(chunks, n_visits, rows, *refs):
    merge_into(chunks, n_visits, rows, refs[:-1], refs[-1])


def last_merge_kernel(chunks, n_visits, rows, starts, *refs):
    out, buffer, sems = refs[-3:]
    done = refs[: len(starts)]
    copies = [
        pltpu.make_async_copy(ref, out.at[:, at : at + ref.shape[1]], sems.at[i])
        for i, (ref, at) in enumerate(zip(done, starts))
    ]
    for copy in copies:
        copy.start()
    merge_into(chunks, n_visits, rows, refs[len(starts) : -3], buffer)
    first = min(c.first for c in chunks) * HD
    copies.append(
        pltpu.make_async_copy(
            buffer, out.at[:, first : first + buffer.shape[1]], sems.at[len(starts)]
        )
    )
    copies[-1].start()
    for copy in copies:
        copy.wait()


def n_stages(count):
    return 3 if count <= 4 else 2


def plan_of(heads, count):
    half, n = heads // 2, n_stages(count)
    sizes = [half // n + (i < half % n) for i in range(n)]
    stages = []
    at = visit_at = 0
    for n in sizes:
        stages.append([Chunk(at, n, True, visit_at), Chunk(at + n, n, False, visit_at)])
        at += 2 * n
        visit_at += n
    return stages


def placement(resident):
    if resident:
        return (
            lambda x: pltpu.with_memory_space_constraint(x, pltpu.VMEM),
            lambda shape, dtype: pltpu.VMEM(shape, dtype),
        )
    return lambda x: x, jax.ShapeDtypeStruct


def on_device(count, queries, keys_now, values_now, keys_stale, values_stale, neighbours):
    rows, width = queries.shape
    assert rows == LANES
    shape = grid_shape(count)
    stages = plan_of(width // HD, count)
    chunks = [c for stage in stages for c in stage]
    assert sum(c.heads for c in chunks) * HD == width and min(c.heads for c in chunks) > 0
    arriving = sum((c.sizes(shape)[1] - 1) * 4 * rows * c.heads * HD * 2 for c in chunks)
    resident = arriving <= VMEM_BUDGET
    in_vmem, result = placement(resident)
    params = pltpu.CompilerParams(vmem_limit_bytes=KERNEL_VMEM if resident else None)
    vmem = pl.BlockSpec(memory_space=pltpu.VMEM)
    in_hbm = pl.BlockSpec(memory_space=pltpu.HBM)

    def gather(moves, sources, shapes, after=()):
        return pl.pallas_call(
            functools.partial(gather_kernel, moves, len(after)),
            in_specs=[vmem if resident else in_hbm] * len(after) + [in_hbm] * len(sources),
            out_specs=[vmem] * len(shapes),
            out_shape=[result(x, jnp.bfloat16) for x in shapes],
            scratch_shapes=[pltpu.SemaphoreType.DMA((len(moves),))],
            compiler_params=params,
            name="gather",
        )(
            *[in_vmem(x) for x in after],
            *[pltpu.with_memory_space_constraint(x, pltpu.HBM) for x in sources],
        )

    by_way = {way: [c for c in chunks if c.across == way] for way in (True, False)}
    moves = [
        (0, c.first * HD, int(way), None, c.visit_at * HD, c.heads * HD)
        for way in (True, False)
        for c in by_way[way]
    ]
    widths = [sum(c.heads for c in by_way[bool(i)]) * HD for i in range(2)]
    mine = gather(moves, [queries], [(rows, w) for w in widths])
    visiting = {}
    for way in (False, True):
        visiting[way] = [mine[int(way)]] + [
            lax.ppermute(mine[int(way)], "reg", pairs_of(count, v, not way, shape))
            for v in range(1, by_way[way][0].sizes(shape)[0])
        ]
    moves = [
        (a, c.first * HD, i, a, 0, c.heads * HD) for i, c in enumerate(chunks) for a in range(4)
    ]
    packed = gather(
        moves,
        [keys_now, values_now, keys_stale, values_stale],
        [(4, rows, c.heads * HD) for c in chunks],
        after=mine,
    )
    shared = {}
    for chunk, pack in zip(chunks, packed):
        shared[chunk] = [pack] + [
            lax.ppermute(pack, "reg", pairs_of(count, s, chunk.across, shape))
            for s in range(1, chunk.sizes(shape)[1])
        ]

    blocks, rules = blocks_of(chunks, count, shape)
    blocks = dict(zip(chunks, blocks))
    table = pl.pallas_call(
        functools.partial(table_kernel, rules, shape),
        in_specs=[pl.BlockSpec(memory_space=pltpu.SMEM)],
        out_specs=vmem,
        out_shape=result((padded(len(rules)), LANES), jnp.float32),
        compiler_params=params,
            name="table",
    )(neighbours.T)

    results = {}
    for stage in [[c] for c in chunks]:
        sizes = [c.sizes(shape) for c in stage]
        operands = [table]
        for chunk in stage:
            operands += visiting[chunk.across] + shared[chunk]
        out_shape = []
        for chunk, (n_visit, _) in zip(stage, sizes):
            out_shape += [
                result((rows, chunk.heads * HD), jnp.bfloat16),
                result((padded(chunk.heads), rows), jnp.float32),
            ]
            out_shape += [result((chunk.message_rows(rows), HD), jnp.bfloat16)] * (n_visit - 1)
        outs = pl.pallas_call(
            functools.partial(attend_kernel, stage, [blocks[c] for c in stage], sizes, rows),
            in_specs=[vmem] * len(operands),
            out_specs=[vmem] * len(out_shape),
            out_shape=out_shape,
            compiler_params=params,
            name="attend",
        )(*[in_vmem(x) for x in operands])
        outs = list(outs)
        for chunk, (n_visit, _) in zip(stage, sizes):
            kept = [outs.pop(0), outs.pop(0)]
            for v in range(1, n_visit):
                pairs = reversed_pairs(pairs_of(count, v, not chunk.across, shape))
                kept.append(lax.ppermute(outs.pop(0), "reg", pairs))
            results[chunk] = [in_vmem(x) for x in kept]

    merged, starts = [], []
    for stage in stages[:-1]:
        operands = [x for c in stage for x in results[c]]
        merged.append(
            pl.pallas_call(
                functools.partial(
                    early_merge_kernel, stage, [c.sizes(shape)[0] for c in stage], rows
                ),
                in_specs=[vmem] * len(operands),
                out_specs=vmem,
                out_shape=result((rows, sum(c.heads for c in stage) * HD), jnp.bfloat16),
                compiler_params=params,
            name="merge",
            )(*operands)
        )
        starts.append(min(c.first for c in stage) * HD)
    stage = stages[-1]
    operands = [x for c in stage for x in results[c]]
    return pl.pallas_call(
        functools.partial(
            last_merge_kernel, stage, [c.sizes(shape)[0] for c in stage], rows, starts
        ),
        in_specs=[vmem] * (len(merged) + len(operands)),
        out_specs=in_hbm,
        out_shape=jax.ShapeDtypeStruct((rows, width), jnp.bfloat16),
        scratch_shapes=[
            pltpu.VMEM((rows, sum(c.heads for c in stage) * HD), jnp.bfloat16),
            pltpu.SemaphoreType.DMA((len(stages),)),
        ],
        compiler_params=params,
            name="finish",
    )(*[in_vmem(x) for x in merged], *operands)


def solution(mesh):
    in_specs = (
        P(("grp", "reg"), None),
        P(("grp", "reg"), None),
        P(("grp", "reg"), None),
        P(("grp", "reg"), None),
        P(("grp", "reg"), None),
        P("grp", None),
    )
    out_specs = P(("grp", "reg"), None)

    def step(*args):
        return on_device(mesh.shape["reg"], *args)

    return jax.shard_map(
        step, mesh=mesh, in_specs=in_specs, out_specs=out_specs, check_vma=False
    )
```

```python
import functools
import math

import jax
import jax.numpy as jnp
from jax import lax
from jax.experimental import pallas as pl
from jax.experimental.pallas import tpu as pltpu
from jax.sharding import PartitionSpec as P


HD = 128
LANES = 128
TILE_ROWS = 16
NEVER = -1e30
VMEM_BUDGET = 2 << 20
KERNEL_VMEM = 2 << 20
SCALE2 = HD**-0.5 * math.log2(math.e)


def grid_shape(count):
    rows = max(d for d in range(1, math.isqrt(count) + 1) if count % d == 0)
    return rows, count // rows


def neighbour_of(region, shift, across, shape):
    rows, cols = shape
    y, x = region // cols, region % cols
    if across:
        return y * cols + (x + shift) % cols
    return ((y + shift) % rows) * cols + x


def pairs_of(count, shift, across, shape):
    return [(neighbour_of(d, shift, across, shape), d) for d in range(count)]


def reversed_pairs(pairs):
    return [(d, s) for s, d in pairs]


def padded(n):
    return -(-n // TILE_ROWS) * TILE_ROWS


class Chunk:
    def __init__(self, first, heads, across, visit_at):
        self.first, self.heads, self.across, self.visit_at = first, heads, across, visit_at

    def sizes(self, shape):
        rows, cols = shape
        return (rows, cols) if self.across else (cols, rows)

    def message_rows(self, rows):
        return self.heads * rows + padded(3 * self.heads)


def gather_kernel(moves, n_after, *refs):
    refs = refs[n_after:]
    n_outs = 1 + max(m[2] for m in moves)
    sources, outs, sems = refs[: -1 - n_outs], refs[-1 - n_outs : -1], refs[-1]
    copies = []
    for i, (source, start, target, layer, at, width) in enumerate(moves):
        to = outs[target] if layer is None else outs[target].at[layer]
        copies.append(
            pltpu.make_async_copy(
                sources[source].at[:, start : start + width],
                to.at[:, at : at + width],
                sems.at[i],
            )
        )
    for copy in copies:
        copy.start()
    for copy in copies:
        copy.wait()


def block_rule(chunk, count, shape, v, s, stale):
    ids = [
        (neighbour_of(d, v, not chunk.across, shape), neighbour_of(d, s, chunk.across, shape))
        for d in range(count)
    ]
    if stale:
        return False if all(q == m for q, m in ids) else True
    close = [abs(q - m) <= 1 for q, m in ids]
    if all(close):
        return None
    return [d for d in range(count) if close[d]] if any(close) else False


def blocks_of(chunks, count, shape):
    entries, rules = [], []
    for chunk in chunks:
        n_visit, n_share = chunk.sizes(shape)
        per_chunk = []
        for v in range(n_visit):
            per_visit = []
            for s in range(n_share):
                for stale in (0, 1):
                    rule = block_rule(chunk, count, shape, v, s, stale)
                    if rule is False:
                        continue
                    key = (chunk.across, v, s, stale, rule)
                    if rule is not None and key not in rules:
                        rules.append(key)
                    per_visit.append((s, stale, None if rule is None else rules.index(key)))
            per_chunk.append(per_visit)
        entries.append(per_chunk)
    return entries, rules


def table_kernel(rules, shape, listed, out):
    region = lax.axis_index("reg")
    for i, (across, v, s, stale, rule) in enumerate(rules):
        if stale:
            query_region = neighbour_of(region, v, not across, shape)
            key_region = neighbour_of(region, s, across, shape)
            hit = listed[0, query_region] == key_region
            for j in range(1, listed.shape[0]):
                hit = hit | (listed[j, query_region] == key_region)
        else:
            hit = functools.reduce(jnp.logical_or, [region == d for d in rule])
        bias = jnp.where(hit, 0.0, NEVER).astype(jnp.float32)
        out[i : i + 1, :] = jnp.full((1, LANES), bias, jnp.float32)


def attend_kernel(chunks, blocks, sizes, rows, *refs):
    refs = list(refs)
    table = refs.pop(0)
    local = {}
    for chunk, (n_visit, n_share) in zip(chunks, sizes):
        local[chunk] = (
            [refs.pop(0) for _ in range(n_visit)],
            [refs.pop(0) for _ in range(n_share)],
        )
    outs = {}
    for chunk, (n_visit, _) in zip(chunks, sizes):
        outs[chunk] = (refs.pop(0), refs.pop(0), [refs.pop(0) for _ in range(n_visit - 1)])
    lane = lax.broadcasted_iota(jnp.int32, (rows, LANES), 1)
    for chunk, plan, (n_visit, n_share) in zip(chunks, blocks, sizes):
        queries, shared = local[chunk]
        out_own, lse_own, messages = outs[chunk]
        heads = chunk.heads
        lse_all = [jnp.zeros((rows, LANES), jnp.float32) for _ in range(n_visit)]
        for h in range(heads):
            there = slice(h * HD, (h + 1) * HD)
            visiting = slice((chunk.visit_at + h) * HD, (chunk.visit_at + h + 1) * HD)
            for v in range(n_visit):
                q = queries[v][:, visiting]
                keys = jnp.concatenate([shared[s][2 * t, :, there] for s, t, _ in plan[v]], axis=0)
                values = jnp.concatenate(
                    [shared[s][2 * t + 1, :, there] for s, t, _ in plan[v]], axis=0
                )
                values = jnp.concatenate(
                    [values, jnp.ones((values.shape[0], LANES), jnp.bfloat16)], axis=1
                )
                scores = lax.dot_general(
                    keys, q, (((1,), (1,)), ((), ())), preferred_element_type=jnp.float32
                )
                pieces = []
                for i, (_, _, line) in enumerate(plan[v]):
                    piece = scores[i * rows : (i + 1) * rows]
                    pieces.append(piece if line is None else piece + table[line : line + 1, :])
                peak = functools.reduce(jnp.maximum, pieces).max(axis=0, keepdims=True) * SCALE2
                weights = [jnp.exp2(p * SCALE2 - peak).astype(jnp.bfloat16) for p in pieces]
                both = lax.dot_general(
                    jnp.concatenate(weights, axis=0),
                    values,
                    (((0,), (0,)), ((), ())),
                    preferred_element_type=jnp.float32,
                )
                total = both[:, HD:]
                out = (both[:, :HD] / total).astype(jnp.bfloat16)
                column = jnp.broadcast_to(peak, (LANES, rows)).T
                lse_all[v] = jnp.where(lane == h, column + jnp.log2(total), lse_all[v])
                if v == 0:
                    out_own[:, there] = out
                else:
                    messages[v - 1][h * rows : (h + 1) * rows, :] = out
        lse_own[...] = lse_all[0].T[: padded(heads)]
        for v in range(1, n_visit):
            flat = lse_all[v].T[: padded(heads)]
            high = flat.astype(jnp.bfloat16).astype(jnp.float32)
            middle = (flat - high).astype(jnp.bfloat16).astype(jnp.float32)
            low = flat - high - middle
            lines = [x[:heads] for x in (high, middle, low)]
            spare = padded(3 * heads) - 3 * heads
            if spare:
                lines.append(jnp.zeros((spare, rows), jnp.float32))
            messages[v - 1][heads * rows :, :] = jnp.concatenate(lines, axis=0).astype(jnp.bfloat16)


def merge_into(chunks, n_visits, rows, refs, buffer):
    first = min(c.first for c in chunks)
    at = 0
    for chunk, n_visit in zip(chunks, n_visits):
        heads = chunk.heads
        part, lse_own = refs[at], refs[at + 1]
        messages = refs[at + 2 : at + 1 + n_visit]
        at += 1 + n_visit
        flats = [lse_own[:heads]]
        for message in messages:
            lines = message[heads * rows :, :].astype(jnp.float32)
            flats.append(
                lines[:heads] + lines[heads : 2 * heads] + lines[2 * heads : 3 * heads]
            )
        top = functools.reduce(jnp.maximum, flats)
        weights = [jnp.exp2(f - top) for f in flats]
        denom = functools.reduce(jnp.add, weights)
        blank = jnp.zeros((LANES - heads, rows), jnp.float32)
        columns = [jnp.concatenate([w / denom, blank], axis=0).T for w in weights]
        for h in range(heads):
            cols = slice(h * HD, (h + 1) * HD)
            parts = [part[:, cols]] + [m[h * rows : (h + 1) * rows, :] for m in messages]
            value = functools.reduce(
                jnp.add,
                [c[:, h : h + 1] * p.astype(jnp.float32) for c, p in zip(columns, parts)],
            )
            to = chunk.first - first + h
            buffer[:, to * HD : (to + 1) * HD] = value.astype(jnp.bfloat16)


def early_merge_kernel(chunks, n_visits, rows, *refs):
    merge_into(chunks, n_visits, rows, refs[:-1], refs[-1])


def last_merge_kernel(chunks, n_visits, rows, starts, *refs):
    out, buffer, sems = refs[-3:]
    done = refs[: len(starts)]
    copies = [
        pltpu.make_async_copy(ref, out.at[:, at : at + ref.shape[1]], sems.at[i])
        for i, (ref, at) in enumerate(zip(done, starts))
    ]
    for copy in copies:
        copy.start()
    merge_into(chunks, n_visits, rows, refs[len(starts) : -3], buffer)
    first = min(c.first for c in chunks) * HD
    copies.append(
        pltpu.make_async_copy(
            buffer, out.at[:, first : first + buffer.shape[1]], sems.at[len(starts)]
        )
    )
    copies[-1].start()
    for copy in copies:
        copy.wait()


def n_stages(count):
    return 3 if count <= 4 else 2


def plan_of(heads, count):
    half, n = heads // 2, n_stages(count)
    sizes = [half // n + (i < half % n) for i in range(n)]
    stages = []
    at = visit_at = 0
    for n in sizes:
        stages.append([Chunk(at, n, True, visit_at), Chunk(at + n, n, False, visit_at)])
        at += 2 * n
        visit_at += n
    return stages


def placement(resident):
    if resident:
        return (
            lambda x: pltpu.with_memory_space_constraint(x, pltpu.VMEM),
            lambda shape, dtype: pltpu.VMEM(shape, dtype),
        )
    return lambda x: x, jax.ShapeDtypeStruct


def on_device(count, queries, keys_now, values_now, keys_stale, values_stale, neighbours):
    rows, width = queries.shape
    assert rows == LANES
    shape = grid_shape(count)
    stages = plan_of(width // HD, count)
    chunks = [c for stage in stages for c in stage]
    assert sum(c.heads for c in chunks) * HD == width and min(c.heads for c in chunks) > 0
    arriving = sum((c.sizes(shape)[1] - 1) * 4 * rows * c.heads * HD * 2 for c in chunks)
    resident = arriving <= VMEM_BUDGET
    in_vmem, result = placement(resident)
    params = pltpu.CompilerParams(vmem_limit_bytes=KERNEL_VMEM if resident else None)
    vmem = pl.BlockSpec(memory_space=pltpu.VMEM)
    in_hbm = pl.BlockSpec(memory_space=pltpu.HBM)

    def gather(moves, sources, shapes, after=()):
        return pl.pallas_call(
            functools.partial(gather_kernel, moves, len(after)),
            in_specs=[vmem if resident else in_hbm] * len(after) + [in_hbm] * len(sources),
            out_specs=[vmem] * len(shapes),
            out_shape=[result(x, jnp.bfloat16) for x in shapes],
            scratch_shapes=[pltpu.SemaphoreType.DMA((len(moves),))],
            compiler_params=params,
            name="gather",
        )(
            *[in_vmem(x) for x in after],
            *[pltpu.with_memory_space_constraint(x, pltpu.HBM) for x in sources],
        )

    by_way = {way: [c for c in chunks if c.across == way] for way in (False, True)}
    first, rest = stages[0], [c for stage in stages[1:] for c in stage]
    keyed = [keys_now, values_now, keys_stale, values_stale]

    def key_moves(some, at, source):
        return [
            (source + a, c.first * HD, at + i, a, 0, c.heads * HD)
            for i, c in enumerate(some)
            for a in range(4)
        ]

    def key_shapes(some):
        return [(4, rows, c.heads * HD) for c in some]

    moves = [
        (0, c.first * HD, int(way), None, c.visit_at * HD, c.heads * HD)
        for way in (False, True)
        for c in by_way[way]
    ]
    widths = [sum(c.heads for c in by_way[way]) * HD for way in (False, True)]
    mine = gather(
        moves + key_moves(first, 2, 1),
        [queries, *keyed],
        [(rows, w) for w in widths] + key_shapes(first),
    )
    mine, packed = mine[:2], mine[2:]
    packed += gather(key_moves(rest, 0, 0), keyed, key_shapes(rest), after=packed[:1])
    visiting = {}
    for way in (False, True):
        visiting[way] = [mine[int(way)]] + [
            lax.ppermute(mine[int(way)], "reg", pairs_of(count, v, not way, shape))
            for v in range(1, by_way[way][0].sizes(shape)[0])
        ]
    shared = {}
    for chunk, pack in zip(chunks, packed):
        shared[chunk] = [pack] + [
            lax.ppermute(pack, "reg", pairs_of(count, s, chunk.across, shape))
            for s in range(1, chunk.sizes(shape)[1])
        ]

    blocks, rules = blocks_of(chunks, count, shape)
    blocks = dict(zip(chunks, blocks))
    table = pl.pallas_call(
        functools.partial(table_kernel, rules, shape),
        in_specs=[pl.BlockSpec(memory_space=pltpu.SMEM)],
        out_specs=vmem,
        out_shape=result((padded(len(rules)), LANES), jnp.float32),
        compiler_params=params,
            name="table",
    )(neighbours.T)

    results = {}
    for stage in [[c] for c in chunks]:
        sizes = [c.sizes(shape) for c in stage]
        operands = [table]
        for chunk in stage:
            operands += visiting[chunk.across] + shared[chunk]
        out_shape = []
        for chunk, (n_visit, _) in zip(stage, sizes):
            out_shape += [
                result((rows, chunk.heads * HD), jnp.bfloat16),
                result((padded(chunk.heads), rows), jnp.float32),
            ]
            out_shape += [result((chunk.message_rows(rows), HD), jnp.bfloat16)] * (n_visit - 1)
        outs = pl.pallas_call(
            functools.partial(attend_kernel, stage, [blocks[c] for c in stage], sizes, rows),
            in_specs=[vmem] * len(operands),
            out_specs=[vmem] * len(out_shape),
            out_shape=out_shape,
            compiler_params=params,
            name="attend",
        )(*[in_vmem(x) for x in operands])
        outs = list(outs)
        for chunk, (n_visit, _) in zip(stage, sizes):
            kept = [outs.pop(0), outs.pop(0)]
            for v in range(1, n_visit):
                pairs = reversed_pairs(pairs_of(count, v, not chunk.across, shape))
                kept.append(lax.ppermute(outs.pop(0), "reg", pairs))
            results[chunk] = [in_vmem(x) for x in kept]

    merged, starts = [], []
    groups = [*stages[:-1], stages[-1][:1], stages[-1][1:]]
    for group in groups[:-1]:
        operands = [x for c in group for x in results[c]]
        merge = pl.pallas_call(
            functools.partial(
                early_merge_kernel, group, [c.sizes(shape)[0] for c in group], rows
            ),
            in_specs=[vmem] * len(operands),
            out_specs=vmem,
            out_shape=result((rows, sum(c.heads for c in group) * HD), jnp.bfloat16),
            compiler_params=params,
            name="merge",
        )
        merged.append(merge(*operands))
        starts.append(min(c.first for c in group) * HD)
    group = groups[-1]
    operands = [x for c in group for x in results[c]]
    return pl.pallas_call(
        functools.partial(
            last_merge_kernel, group, [c.sizes(shape)[0] for c in group], rows, starts
        ),
        in_specs=[vmem] * (len(merged) + len(operands)),
        out_specs=in_hbm,
        out_shape=jax.ShapeDtypeStruct((rows, width), jnp.bfloat16),
        scratch_shapes=[
            pltpu.VMEM((rows, sum(c.heads for c in group) * HD), jnp.bfloat16),
            pltpu.SemaphoreType.DMA((len(groups),)),
        ],
        compiler_params=params,
        name="finish",
    )(*[in_vmem(x) for x in merged], *operands)


def solution(mesh):
    in_specs = (
        P(("grp", "reg"), None),
        P(("grp", "reg"), None),
        P(("grp", "reg"), None),
        P(("grp", "reg"), None),
        P(("grp", "reg"), None),
        P("grp", None),
    )
    out_specs = P(("grp", "reg"), None)

    def step(*args):
        return on_device(mesh.shape["reg"], *args)

    return jax.shard_map(
        step, mesh=mesh, in_specs=in_specs, out_specs=out_specs, check_vma=False
    )
```
